32 devices in a mesh: rec: 4 (over x, core), tm: 8 (over z, y).
Axes of the slice: x: 2, y: 2, z: 4, core: 2. Of those that a mesh axis runs over, the one named last changes fastest.
Arguments:
- signal: bfloat16 [8192, 1280], P(('rec', 'tm')), parts along dimension 0, may hold values from -6 to 6
- position_kernel: bfloat16 [1280, 80, 128], P('tm'), may hold values from -0.0625 to 0.0625
- position_bias: float32 [1280], P('tm'), may hold values from -3 to 3
- layer_gain: float32 [1280], replicated, may hold values from 0.5 to 1.5
- layer_shift: float32 [1280], replicated, may hold values from -3 to 3
- query_weight: bfloat16 [1280, 640], P('tm'), may hold values from -0.25 to 0.25
- query_bias: float32 [640], replicated, may hold values from -4 to 4
- key_weight: bfloat16 [1280, 640], P('tm'), may hold values from -0.25 to 0.25
- value_weight: bfloat16 [1280, 640], P('tm'), may hold values from -0.15625 to 0.15625
- value_bias: float32 [640], replicated, may hold values from -3 to 3
- output_weight: bfloat16 [640, 1280], P(None, 'tm'), may hold values from -0.25 to 0.25
- output_bias: float32 [1280], replicated, may hold values from -3 to 3
- key_blocks: int32 [64, 5], P(('rec', 'tm')), parts along dimension 0, may hold values from -1 to 15, as said below
- global_blocks: int32 [16], P('rec'), parts along dimension 0, may hold values from 0 to 15, as said below
Outputs:
- encoded: bfloat16 [8192, 1280], P(('rec', 'tm')), parts along dimension 0
The draws below stay inside these ranges and needn't reach their ends.
There are 4 independent parts, one for each index of `rec`. The reference program is written for one: setup_inputs(seed, part) draws one part's arguments, and reference() takes and returns one part's arrays. A program takes and returns all parts, laid end to end along the dimension named above; an argument that names none is the same for every part. Nothing has to cross between parts.
Inputs may be any that keep to these rules, and one draw needn't show every extreme that they name: `key_blocks`: row b lists distinct blocks in any order, padded with -1; it always holds b itself, and otherwise only blocks c with |c - b| <= 2 that lie in b's segment, segments being runs of consecutive blocks of the recording. `global_blocks`: 4 distinct block numbers of the recording.
All inputs are finite; a program needn't handle non-finite values.
Results may differ from the reference program's by a relative error of at most 0.0055.
Values may be sent and summed in bfloat16 or wider, within the bound.
A program may use at most 128 MiB of HBM per device.

```python
import math
import jax
import jax.numpy as jnp
from jax import lax

D = 1280
GROUPS = 16
KERNEL = 128
HEAD = 80
HEADS = 8
BLOCK = 128
WIN = 2
GLOBALS = 4
GW = 80
FRAMES = 2048
NQB = 16


def draw_query_weight(key, part):
    full = jax.random.normal(jax.random.fold_in(key, 1), (D, HEADS * HEAD), jnp.float32) * (3.0 * D ** (-0.5))
    return jnp.clip(full, -0.25, 0.25).astype(jnp.bfloat16)


def draw_key_weight(key, part):
    full = jax.random.normal(jax.random.fold_in(key, 2), (D, HEADS * HEAD), jnp.float32) * D ** (-0.5)
    return jnp.clip(full, -0.25, 0.25).astype(jnp.bfloat16)


def draw_key_blocks(key, part):
    span = 2 * WIN + 1
    block = jnp.arange(NQB, dtype=jnp.int32)
    cuts = (jax.random.randint(jax.random.fold_in(key, 11), (NQB,), 0, 4) == 0) & (block > span)
    segment = jnp.cumsum(cuts.astype(jnp.int32))
    nearby = block[:, None] + jnp.arange(span, dtype=jnp.int32)[None, :] - WIN
    inside = (nearby >= 0) & (nearby < NQB)
    clamped = jnp.clip(nearby, 0, NQB - 1)
    same = inside & (segment[clamped] == segment[:, None])
    listed = jnp.where(same, nearby, -1)
    ranks = jax.random.randint(jax.random.fold_in(key, 12), (NQB, span), 0, 1 << 20) * span + jnp.arange(span, dtype=jnp.int32)[None, :]
    order = jnp.argsort(ranks, axis=1)
    return jnp.take_along_axis(listed, order, axis=1).astype(jnp.int32)


def draw_global_blocks(key, part):
    return jax.random.permutation(jax.random.fold_in(key, 13), NQB)[:GLOBALS].astype(jnp.int32)


def shard_levels(key, extent, cuts, least, high):
    level, own = 1.0, jax.random.fold_in(key, 6)
    for axis_at, parts in cuts:
        steps = jnp.exp(jax.random.uniform(jax.random.fold_in(own, axis_at), (parts,), jnp.float32, least / len(cuts), high / len(cuts)))
        level = level * jnp.repeat(steps, extent[axis_at] // parts).reshape([-1 if axis == axis_at else 1 for axis in range(len(extent))])
    return level


def gaussian(stream_key, extent, spread, limit, cuts=(), kind=jnp.bfloat16):
    factor_of = shard_levels(stream_key, extent, cuts, -0.22, 0.18) if cuts else 1.0
    result = jax.random.normal(stream_key, extent, jnp.float32) * spread * factor_of
    return jnp.minimum(jnp.maximum(result, -limit), limit).astype(kind)


def setup_inputs(seed: int = 0, part: int = 0) -> dict:
    key_list = jax.random.split(jax.random.key(seed), 15)
    own_keys = jax.random.split(jax.random.fold_in(key_list[14], part), 15)
    return {
        "signal": gaussian(own_keys[0], (FRAMES, D), 1.0, 6.0, ((0, 8),)),
        "position_kernel": gaussian(key_list[1], (D, GW, KERNEL), (GW * KERNEL) ** -0.5, 0.0625, ((0, 8),)),
        "position_bias": gaussian(key_list[2], (D,), 0.5, 3.0, ((0, 8),), jnp.float32),
        "layer_gain": jnp.clip(jax.random.uniform(key_list[3], (D,), jnp.float32, 0.5, 1.5), 0.5, 1.5),
        "layer_shift": gaussian(key_list[4], (D,), 0.5, 3.0, (), jnp.float32),
        "query_weight": draw_query_weight(jax.random.fold_in(key_list[14], 71), part),
        "query_bias": gaussian(key_list[6], (HEADS * HEAD,), 1.0, 4.0, (), jnp.float32),
        "key_weight": draw_key_weight(jax.random.fold_in(key_list[14], 71), part),
        "value_weight": gaussian(key_list[8], (D, HEADS * HEAD), D ** -0.5, 0.15625, ((0, 8),)),
        "value_bias": gaussian(key_list[9], (HEADS * HEAD,), 0.5, 3.0, (), jnp.float32),
        "output_weight": gaussian(key_list[10], (HEADS * HEAD, D), (HEADS * HEAD) ** -0.5, 0.25, ((1, 8),)),
        "output_bias": gaussian(key_list[11], (D,), 0.5, 3.0, (), jnp.float32),
        "key_blocks": draw_key_blocks(jax.random.fold_in(jax.random.fold_in(key_list[14], part), 71), part),
        "global_blocks": draw_global_blocks(jax.random.fold_in(jax.random.fold_in(key_list[14], part), 71), part),
    }


EPSILON = 1e-05

def attend(queries, key_rows, value_rows, allowed):
    block_count, row_count, heads_width = queries.shape
    query_heads = queries.reshape(block_count, row_count, HEADS, HEAD).astype(jnp.float32)
    key_heads = key_rows.reshape(block_count, key_rows.shape[1], HEADS, HEAD).astype(jnp.float32)
    value_heads = value_rows.reshape(block_count, value_rows.shape[1], HEADS, HEAD).astype(jnp.float32)
    scores = jnp.einsum('bqhe,bkhe->bhqk', query_heads, key_heads, precision=lax.Precision.HIGHEST) * (1.0 / math.sqrt(HEAD))
    scores = jnp.where(allowed[:, None, None, :], scores, -jnp.inf)
    row_max = lax.optimization_barrier(jnp.max(scores, axis=-1, keepdims=True))
    weights = jnp.exp(scores - row_max)
    row_total = lax.optimization_barrier(jnp.sum(weights, axis=-1))
    probability = weights.astype(jnp.bfloat16).astype(jnp.float32)
    context_sum = jnp.einsum('bhqk,bkhe->bqhe', probability, value_heads, precision=lax.Precision.HIGHEST)
    context = context_sum / jnp.transpose(row_total, (0, 2, 1))[..., None]
    return context.reshape(block_count, row_count, heads_width).astype(jnp.bfloat16)

def reference(signal, position_kernel, position_bias, layer_gain, layer_shift, query_weight, query_bias, key_weight, value_weight, value_bias, output_weight, output_bias, key_blocks, global_blocks):
    stacked = signal.astype(jnp.float32).T[None]
    kernels = position_kernel.astype(jnp.float32)
    response = lax.conv_general_dilated(stacked, kernels, (1,), [(KERNEL // 2, KERNEL // 2 - 1)], dimension_numbers=('NCH', 'OIH', 'NCH'), feature_group_count=GROUPS, precision=lax.Precision.HIGHEST)[0]
    position = jax.nn.gelu(response + position_bias[:, None], approximate=False).astype(jnp.bfloat16)
    hidden = signal.astype(jnp.float32) + position.T.astype(jnp.float32)
    average = lax.optimization_barrier(jnp.mean(hidden, axis=-1, keepdims=True))
    centered = hidden - average
    variance = lax.optimization_barrier(jnp.mean(centered * centered, axis=-1, keepdims=True))
    normed = (centered * lax.rsqrt(variance + EPSILON) * layer_gain + layer_shift).astype(jnp.bfloat16)
    queries = (jnp.dot(normed, query_weight, preferred_element_type=jnp.float32) + query_bias).astype(jnp.bfloat16)
    keys = jnp.dot(normed, key_weight, preferred_element_type=jnp.float32).astype(jnp.bfloat16)
    values = (jnp.dot(normed, value_weight, preferred_element_type=jnp.float32) + value_bias).astype(jnp.bfloat16)
    heads_width = HEADS * HEAD
    block_ids = jnp.concatenate([key_blocks, jnp.broadcast_to(global_blocks[None, :], (NQB, GLOBALS))], axis=1)
    repeated = jnp.any(global_blocks[None, :, None] == key_blocks[:, None, :], axis=-1)
    allowed = jnp.concatenate([key_blocks >= 0, jnp.logical_not(repeated)], axis=1)
    key_table = keys.reshape(NQB, BLOCK, heads_width)
    value_table = values.reshape(NQB, BLOCK, heads_width)
    query_table = queries.reshape(NQB, BLOCK, heads_width)

    def one_block(operands):
        query_block, identifiers, permitted = operands
        clamped = jnp.maximum(identifiers, 0).astype(jnp.int32)
        key_rows = key_table[clamped].reshape(1, -1, heads_width)
        value_rows = value_table[clamped].reshape(1, -1, heads_width)
        return attend(query_block[None], key_rows, value_rows, jnp.repeat(permitted, BLOCK)[None])[0]
    context = lax.map(one_block, (query_table, block_ids, allowed)).reshape(FRAMES, heads_width)
    projected = jnp.dot(context, output_weight, preferred_element_type=jnp.float32)
    return (hidden + projected + output_bias).astype(jnp.bfloat16)
```

```python
import math

import jax
import jax.numpy as jnp
import numpy as np
from jax import lax
from jax.experimental import pallas as pl
from jax.experimental.pallas import tpu as pltpu
from jax.sharding import PartitionSpec as P

HEAD = 80
HEADS = 8
BLOCK = 128
GLOBALS = 4


EPSILON = 1e-05


def attend(queries, key_rows, value_rows, allowed):
    block_count, row_count, heads_width = queries.shape
    query_heads = queries.reshape(block_count, row_count, HEADS, HEAD)
    key_heads = key_rows.reshape(block_count, key_rows.shape[1], HEADS, HEAD)
    value_heads = value_rows.reshape(block_count, value_rows.shape[1], HEADS, HEAD)
    scores = jnp.einsum(
        "bqhe,bkhe->bhqk", query_heads, key_heads, preferred_element_type=jnp.float32
    ) * (1.0 / math.sqrt(HEAD))
    scores = jnp.where(allowed[:, None, None, :], scores, -jnp.inf)
    row_max = jnp.max(scores, axis=-1, keepdims=True)
    weights = jnp.exp(scores - row_max)
    row_total = jnp.sum(weights, axis=-1)
    probability = weights.astype(jnp.bfloat16)
    context_sum = jnp.einsum(
        "bhqk,bkhe->bqhe", probability, value_heads, preferred_element_type=jnp.float32
    )
    context = context_sum / jnp.transpose(row_total, (0, 2, 1))[..., None]
    return context.reshape(block_count, row_count, heads_width).astype(jnp.bfloat16)


def general(
    signal,
    position_kernel,
    position_bias,
    layer_gain,
    layer_shift,
    query_weight,
    query_bias,
    key_weight,
    value_weight,
    value_bias,
    output_weight,
    output_bias,
    key_blocks,
    global_blocks,
):
    devices = lax.axis_size("tm")
    frame_count, model_width = signal.shape
    channel_share, group_width, kernel_taps = position_kernel.shape
    inner_width = max(channel_share, group_width)
    folded = signal.T
    if channel_share >= group_width:
        outgoing = folded.reshape(devices, channel_share, frame_count)
    else:
        start_groups = np.arange(devices) * channel_share // group_width
        outgoing = jnp.take(
            folded.reshape(model_width // group_width, group_width, frame_count),
            start_groups,
            axis=0,
        )
    incoming = lax.all_to_all(outgoing, "tm", split_axis=0, concat_axis=2, tiled=True)
    response = lax.conv_general_dilated(
        incoming,
        position_kernel,
        (1,),
        [(kernel_taps // 2, kernel_taps // 2 - 1)],
        dimension_numbers=("NCH", "OIH", "NCH"),
        feature_group_count=inner_width // group_width,
        preferred_element_type=jnp.float32,
    )[0]
    position = jax.nn.gelu(response + position_bias[:, None], approximate=False).astype(
        jnp.bfloat16
    )
    returned = lax.all_to_all(position, "tm", split_axis=1, concat_axis=0, tiled=True)
    hidden = signal.astype(jnp.float32) + returned.T.astype(jnp.float32)
    average = jnp.mean(hidden, axis=-1, keepdims=True)
    centered = hidden - average
    variance = jnp.mean(centered * centered, axis=-1, keepdims=True)
    normed = (centered * lax.rsqrt(variance + EPSILON) * layer_gain + layer_shift).astype(
        jnp.bfloat16
    )
    heads_width = query_weight.shape[1]
    zero_sums = jnp.zeros((frame_count, heads_width), jnp.float32)
    totals = (zero_sums, zero_sums, zero_sums)
    pieces = (
        lax.all_gather(query_weight, "tm", axis=0, tiled=True),
        lax.all_gather(key_weight, "tm", axis=0, tiled=True),
        lax.all_gather(value_weight, "tm", axis=0, tiled=True),
    )
    columns = lax.slice_in_dim(normed, 0, pieces[0].shape[0], axis=1)
    query_sum, key_sum, value_sum = tuple(
        (
            running + jnp.dot(columns, weight_rows, preferred_element_type=jnp.float32)
            for running, weight_rows in zip(totals, pieces)
        )
    )
    queries = (query_sum + query_bias).astype(jnp.bfloat16)
    key_part = key_sum.astype(jnp.bfloat16)
    value_part = (value_sum + value_bias).astype(jnp.bfloat16)
    key_value = jnp.stack((key_part, value_part), axis=1)
    per_device = frame_count // BLOCK
    repeated = jnp.any(global_blocks[None, :, None] == key_blocks[:, None, :], axis=-1)
    whole = lax.all_gather(key_value, "tm", axis=0, tiled=True)
    block_ids = jnp.concatenate(
        [key_blocks, jnp.broadcast_to(global_blocks[None, :], (per_device, GLOBALS))], axis=1
    )
    allowed = jnp.concatenate([key_blocks >= 0, jnp.logical_not(repeated)], axis=1)
    candidates = whole.reshape(-1, BLOCK, 2, heads_width)[jnp.maximum(block_ids, 0)]
    key_rows = candidates[:, :, :, 0].reshape(per_device, -1, heads_width)
    value_rows = candidates[:, :, :, 1].reshape(per_device, -1, heads_width)
    allowed_rows = jnp.repeat(allowed, BLOCK, axis=1)
    context = attend(
        queries.reshape(per_device, BLOCK, heads_width), key_rows, value_rows, allowed_rows
    ).reshape(frame_count, heads_width)
    projected = jnp.dot(
        context,
        lax.all_gather(output_weight, "tm", axis=1, tiled=True),
        preferred_element_type=jnp.float32,
    )
    return (hidden + projected + output_bias).astype(jnp.bfloat16)


PHASES = 3
LANES = 256
STEP = 4


def conv_kernel(rows, steps, x_ref, w_ref, o_ref):
    o_ref[0] = jnp.zeros_like(o_ref[0])

    for step in range(0, steps, STEP):
        window = jnp.concatenate(
            [
                x_ref[0, step + at : step + at + rows, :].astype(jnp.bfloat16)
                for at in range(STEP)
            ],
            axis=1,
        )
        taps = w_ref[0, step : step + STEP].reshape(STEP * LANES, LANES)
        o_ref[0] += jnp.dot(window, taps, preferred_element_type=jnp.float32)


def position_term(incoming, position_kernel, position_bias):
    frames, channels = incoming.shape
    _, width, taps = position_kernel.shape
    groups = channels // width
    reach = taps // 2
    lead = -(-reach // PHASES)
    shift = lead * PHASES - reach
    steps = -(-(taps + shift + PHASES - 1) // (PHASES * STEP)) * STEP
    rows = -(-frames // PHASES)
    rows_padded = -(-rows // 16) * 16
    total_rows = -(-(rows_padded + steps) // 8) * 8
    front = lead * PHASES
    inner = PHASES * width
    spread = jnp.pad(incoming, ((front, total_rows * PHASES - front - frames), (0, 0)))
    spread = spread.reshape(total_rows, PHASES, groups, width)
    spread = spread.transpose(2, 0, 1, 3).reshape(groups, total_rows, inner)
    spread = jnp.pad(spread, ((0, 0), (0, 0), (0, LANES - inner))).astype(jnp.float32)
    kernels = position_kernel.reshape(groups, width, width, taps).transpose(0, 3, 2, 1)
    span = steps * PHASES
    matrix = jnp.concatenate(
        [
            jnp.pad(
                kernels,
                ((0, 0), (shift + phase, span - taps - shift - phase), (0, 0), (0, 0)),
            )
            for phase in range(PHASES)
        ],
        axis=3,
    ).reshape(groups, steps, inner, inner)
    matrix = jnp.pad(matrix, ((0, 0), (0, 0), (0, LANES - inner), (0, LANES - inner)))
    response = pl.pallas_call(
        lambda *refs: conv_kernel(rows_padded, steps, *refs),
        out_shape=jax.ShapeDtypeStruct((groups, rows_padded, LANES), jnp.float32),
        grid=(groups,),
        in_specs=[
            pl.BlockSpec((1, total_rows, LANES), lambda g: (g, 0, 0)),
            pl.BlockSpec((1, steps, LANES, LANES), lambda g: (g, 0, 0, 0)),
        ],
        out_specs=pl.BlockSpec((1, rows_padded, LANES), lambda g: (g, 0, 0)),
        compiler_params=pltpu.CompilerParams(vmem_limit_bytes=40 * 1024 * 1024),
    )(spread, matrix)
    biases = jnp.tile(position_bias.reshape(groups, 1, width), (1, 1, PHASES))
    position = jax.nn.gelu(response[:, :rows, :inner] + biases, approximate=False)
    position = position.astype(jnp.bfloat16).reshape(groups, rows * PHASES, width)
    return position[:, :frames].transpose(1, 0, 2).reshape(frames, channels)


def attention_kernel(listed, scale, ids_ref, mask_ref, q_ref, k_ref, v_ref, o_ref):
    row = pl.program_id(0)
    queries = q_ref[...]
    scores, values = [], []
    for at in range(listed):
        begin = pl.multiple_of(ids_ref[row, at] * BLOCK, BLOCK)
        score = lax.dot_general(
            queries,
            k_ref[pl.ds(begin, BLOCK), :],
            (((1,), (1,)), ((), ())),
            preferred_element_type=jnp.float32,
        )
        scores.append(jnp.where(mask_ref[row, at] > 0, score * scale, -jnp.inf))
        values.append(v_ref[pl.ds(begin, BLOCK), :])
    peak = scores[0]
    for score in scores[1:]:
        peak = jnp.maximum(peak, score)
    peak = jnp.max(peak, axis=1, keepdims=True)
    weights = [jnp.exp(score - peak) for score in scores]
    total = weights[0]
    for weight in weights[1:]:
        total = total + weight
    total = jnp.sum(total, axis=1, keepdims=True)
    probability = jnp.concatenate([weight.astype(jnp.bfloat16) for weight in weights], axis=1)
    context = jnp.dot(
        probability, jnp.concatenate(values, axis=0), preferred_element_type=jnp.float32
    )
    o_ref[...] = (context / total).astype(jnp.bfloat16)


def attend_head(queries, keys, values, block_ids, allowed):
    frames, width = queries.shape
    blocks, listed = block_ids.shape
    whole = pl.BlockSpec((frames, width), lambda b, *_: (0, 0))
    tile = pl.BlockSpec((BLOCK, width), lambda b, *_: (b, 0))
    return pl.pallas_call(
        lambda *refs: attention_kernel(listed, 1.0 / math.sqrt(HEAD), *refs),
        out_shape=jax.ShapeDtypeStruct((frames, width), jnp.bfloat16),
        grid_spec=pltpu.PrefetchScalarGridSpec(
            num_scalar_prefetch=2,
            grid=(blocks,),
            in_specs=[tile, whole, whole],
            out_specs=tile,
        ),
    )(block_ids, allowed, queries, keys, values)


def by_heads(
    signal,
    position_kernel,
    position_bias,
    layer_gain,
    layer_shift,
    query_weight,
    query_bias,
    key_weight,
    value_weight,
    value_bias,
    output_weight,
    output_bias,
    key_blocks,
    global_blocks,
):
    records = lax.axis_size("rec")
    record = lax.axis_index("rec")
    share = query_weight.shape[0]
    part = share // records
    inner = HEADS * HEAD
    stacked = jnp.stack((query_weight, key_weight, value_weight), axis=1)
    stacked = stacked.reshape(share, 3, HEADS, HEAD).transpose(0, 2, 1, 3)
    stacked = jnp.concatenate((stacked.reshape(share, 3 * inner), output_weight.T), axis=1)
    mine = lax.dynamic_slice_in_dim(stacked, record * part, part, axis=0)

    incoming = lax.all_to_all(signal, "tm", split_axis=1, concat_axis=0, tiled=True)
    weights = lax.all_gather(mine, ("tm", "rec"), axis=0, tiled=True)
    listed = lax.all_gather(key_blocks, "tm", axis=0, tiled=True)
    position = position_term(incoming, position_kernel, position_bias)
    returned = lax.all_to_all(position, "tm", split_axis=0, concat_axis=1, tiled=True)
    hidden = signal.astype(jnp.float32) + returned.astype(jnp.float32)
    average = jnp.mean(hidden, axis=-1, keepdims=True)
    centered = hidden - average
    variance = jnp.mean(centered * centered, axis=-1, keepdims=True)
    normed = (centered * lax.rsqrt(variance + EPSILON) * layer_gain + layer_shift).astype(
        jnp.bfloat16
    )
    biases = jnp.stack((query_bias, jnp.zeros_like(query_bias), value_bias))
    biases = biases.reshape(3, HEADS, HEAD).transpose(1, 0, 2).reshape(-1)
    projected = jnp.dot(normed, weights[:, : 3 * inner], preferred_element_type=jnp.float32)
    projected = (projected + biases).astype(jnp.bfloat16)
    headed = lax.all_to_all(projected, "tm", split_axis=1, concat_axis=0, tiled=True)
    blocks = listed.shape[0]
    repeated = jnp.any(global_blocks[None, :, None] == listed[:, None, :], axis=-1)
    block_ids = jnp.concatenate(
        [jnp.maximum(listed, 0), jnp.broadcast_to(global_blocks[None, :], (blocks, GLOBALS))],
        axis=1,
    )
    allowed = jnp.concatenate([listed >= 0, jnp.logical_not(repeated)], axis=1)
    context = attend_head(
        headed[:, :HEAD],
        headed[:, HEAD : 2 * HEAD],
        headed[:, 2 * HEAD :],
        block_ids,
        allowed.astype(jnp.int32),
    )
    context = lax.all_to_all(context, "tm", split_axis=0, concat_axis=1, tiled=True)
    projected = lax.dot_general(
        context,
        weights[:, 3 * inner :],
        (((1,), (1,)), ((), ())),
        preferred_element_type=jnp.float32,
    )
    return (hidden + projected + output_bias).astype(jnp.bfloat16)


def body(*operands):
    share, width, _ = operands[1].shape
    fits = lax.axis_size("tm") == HEADS and share % width == 0
    fits = fits and operands[5].shape[0] % lax.axis_size("rec") == 0
    return (by_heads if fits else general)(*operands)


def solution(mesh):
    placed = (
        P(("rec", "tm"), None),
        P("tm", None, None),
        P("tm"),
        P(),
        P(),
        P("tm", None),
        P(),
        P("tm", None),
        P("tm", None),
        P(),
        P(None, "tm"),
        P(),
        P(("rec", "tm"), None),
        P("rec"),
    )
    return jax.shard_map(
        body, mesh=mesh, in_specs=placed, out_specs=P(("rec", "tm"), None), check_vma=False
    )
```

```python
import math

import jax
import jax.numpy as jnp
import numpy as np
from jax import lax
from jax.experimental import pallas as pl
from jax.experimental.pallas import tpu as pltpu
from jax.sharding import PartitionSpec as P

HEAD = 80
HEADS = 8
BLOCK = 128
GLOBALS = 4


EPSILON = 1e-05


def attend(queries, key_rows, value_rows, allowed):
    block_count, row_count, heads_width = queries.shape
    query_heads = queries.reshape(block_count, row_count, HEADS, HEAD)
    key_heads = key_rows.reshape(block_count, key_rows.shape[1], HEADS, HEAD)
    value_heads = value_rows.reshape(block_count, value_rows.shape[1], HEADS, HEAD)
    scores = jnp.einsum(
        "bqhe,bkhe->bhqk", query_heads, key_heads, preferred_element_type=jnp.float32
    ) * (1.0 / math.sqrt(HEAD))
    scores = jnp.where(allowed[:, None, None, :], scores, -jnp.inf)
    row_max = jnp.max(scores, axis=-1, keepdims=True)
    weights = jnp.exp(scores - row_max)
    row_total = jnp.sum(weights, axis=-1)
    probability = weights.astype(jnp.bfloat16)
    context_sum = jnp.einsum(
        "bhqk,bkhe->bqhe", probability, value_heads, preferred_element_type=jnp.float32
    )
    context = context_sum / jnp.transpose(row_total, (0, 2, 1))[..., None]
    return context.reshape(block_count, row_count, heads_width).astype(jnp.bfloat16)


def general(
    signal,
    position_kernel,
    position_bias,
    layer_gain,
    layer_shift,
    query_weight,
    query_bias,
    key_weight,
    value_weight,
    value_bias,
    output_weight,
    output_bias,
    key_blocks,
    global_blocks,
):
    devices = lax.axis_size("tm")
    frame_count, model_width = signal.shape
    channel_share, group_width, kernel_taps = position_kernel.shape
    inner_width = max(channel_share, group_width)
    folded = signal.T
    if channel_share >= group_width:
        outgoing = folded.reshape(devices, channel_share, frame_count)
    else:
        start_groups = np.arange(devices) * channel_share // group_width
        outgoing = jnp.take(
            folded.reshape(model_width // group_width, group_width, frame_count),
            start_groups,
            axis=0,
        )
    incoming = lax.all_to_all(outgoing, "tm", split_axis=0, concat_axis=2, tiled=True)
    response = lax.conv_general_dilated(
        incoming,
        position_kernel,
        (1,),
        [(kernel_taps // 2, kernel_taps // 2 - 1)],
        dimension_numbers=("NCH", "OIH", "NCH"),
        feature_group_count=inner_width // group_width,
        preferred_element_type=jnp.float32,
    )[0]
    position = jax.nn.gelu(response + position_bias[:, None], approximate=False).astype(
        jnp.bfloat16
    )
    returned = lax.all_to_all(position, "tm", split_axis=1, concat_axis=0, tiled=True)
    hidden = signal.astype(jnp.float32) + returned.T.astype(jnp.float32)
    average = jnp.mean(hidden, axis=-1, keepdims=True)
    centered = hidden - average
    variance = jnp.mean(centered * centered, axis=-1, keepdims=True)
    normed = (centered * lax.rsqrt(variance + EPSILON) * layer_gain + layer_shift).astype(
        jnp.bfloat16
    )
    heads_width = query_weight.shape[1]
    zero_sums = jnp.zeros((frame_count, heads_width), jnp.float32)
    totals = (zero_sums, zero_sums, zero_sums)
    pieces = (
        lax.all_gather(query_weight, "tm", axis=0, tiled=True),
        lax.all_gather(key_weight, "tm", axis=0, tiled=True),
        lax.all_gather(value_weight, "tm", axis=0, tiled=True),
    )
    columns = lax.slice_in_dim(normed, 0, pieces[0].shape[0], axis=1)
    query_sum, key_sum, value_sum = tuple(
        (
            running + jnp.dot(columns, weight_rows, preferred_element_type=jnp.float32)
            for running, weight_rows in zip(totals, pieces)
        )
    )
    queries = (query_sum + query_bias).astype(jnp.bfloat16)
    key_part = key_sum.astype(jnp.bfloat16)
    value_part = (value_sum + value_bias).astype(jnp.bfloat16)
    key_value = jnp.stack((key_part, value_part), axis=1)
    per_device = frame_count // BLOCK
    repeated = jnp.any(global_blocks[None, :, None] == key_blocks[:, None, :], axis=-1)
    whole = lax.all_gather(key_value, "tm", axis=0, tiled=True)
    block_ids = jnp.concatenate(
        [key_blocks, jnp.broadcast_to(global_blocks[None, :], (per_device, GLOBALS))], axis=1
    )
    allowed = jnp.concatenate([key_blocks >= 0, jnp.logical_not(repeated)], axis=1)
    candidates = whole.reshape(-1, BLOCK, 2, heads_width)[jnp.maximum(block_ids, 0)]
    key_rows = candidates[:, :, :, 0].reshape(per_device, -1, heads_width)
    value_rows = candidates[:, :, :, 1].reshape(per_device, -1, heads_width)
    allowed_rows = jnp.repeat(allowed, BLOCK, axis=1)
    context = attend(
        queries.reshape(per_device, BLOCK, heads_width), key_rows, value_rows, allowed_rows
    ).reshape(frame_count, heads_width)
    projected = jnp.dot(
        context,
        lax.all_gather(output_weight, "tm", axis=1, tiled=True),
        preferred_element_type=jnp.float32,
    )
    return (hidden + projected + output_bias).astype(jnp.bfloat16)


PHASES = 3
LANES = 256
STEP = 4


def expand_kernel(taps, width, shift, steps, k_ref, o_ref):
    inner = PHASES * width
    for step in range(steps):
        columns = []
        for phase in range(PHASES):
            begin = step * PHASES - phase - shift
            low = min(max(begin, 0), taps)
            high = min(max(begin + PHASES, 0), taps)
            pieces = []
            if low > begin and high > low:
                pieces.append(jnp.zeros(((low - begin) * width, width), jnp.bfloat16))
            if high > low:
                pieces.append(k_ref[0, low * width : high * width, :])
            missing = inner - sum(piece.shape[0] for piece in pieces)
            if missing:
                pieces.append(jnp.zeros((missing, width), jnp.bfloat16))
            columns.append(pieces[0] if len(pieces) == 1 else jnp.concatenate(pieces, axis=0))
        columns.append(jnp.zeros((inner, LANES - inner), jnp.bfloat16))
        o_ref[0, step, :inner, :] = jnp.concatenate(columns, axis=1)
        o_ref[0, step, inner:, :] = jnp.zeros((LANES - inner, LANES), jnp.bfloat16)


def conv_kernel(rows, steps, x_ref, w_ref, o_ref):
    o_ref[0] = jnp.zeros_like(o_ref[0])

    for step in range(0, steps, STEP):
        window = jnp.concatenate(
            [
                x_ref[0, step + at : step + at + rows, :].astype(jnp.bfloat16)
                for at in range(STEP)
            ],
            axis=1,
        )
        taps = w_ref[0, step : step + STEP].reshape(STEP * LANES, LANES)
        o_ref[0] += jnp.dot(window, taps, preferred_element_type=jnp.float32)


def position_term(incoming, position_kernel, position_bias):
    frames, channels = incoming.shape
    _, width, taps = position_kernel.shape
    groups = channels // width
    reach = taps // 2
    lead = -(-reach // PHASES)
    shift = lead * PHASES - reach
    steps = -(-(taps + shift + PHASES - 1) // (PHASES * STEP)) * STEP
    rows = -(-frames // PHASES)
    rows_padded = -(-rows // 16) * 16
    total_rows = -(-(rows_padded + steps) // 8) * 8
    front = lead * PHASES
    inner = PHASES * width
    spread = jnp.pad(incoming, ((front, total_rows * PHASES - front - frames), (0, 0)))
    spread = spread.reshape(total_rows, PHASES, groups, width)
    spread = spread.transpose(2, 0, 1, 3).reshape(groups, total_rows, inner)
    spread = jnp.pad(spread, ((0, 0), (0, 0), (0, LANES - inner))).astype(jnp.float32)
    kernels = position_kernel.reshape(groups, width, width, taps).transpose(0, 3, 2, 1)
    kernels = kernels.reshape(groups, taps * width, width)
    matrix = pl.pallas_call(
        lambda *refs: expand_kernel(taps, width, shift, steps, *refs),
        out_shape=jax.ShapeDtypeStruct((groups, steps, LANES, LANES), jnp.bfloat16),
        grid=(groups,),
        in_specs=[pl.BlockSpec((1, taps * width, width), lambda g: (g, 0, 0))],
        out_specs=pl.BlockSpec((1, steps, LANES, LANES), lambda g: (g, 0, 0, 0)),
        compiler_params=pltpu.CompilerParams(vmem_limit_bytes=40 * 1024 * 1024),
    )(kernels)
    response = pl.pallas_call(
        lambda *refs: conv_kernel(rows_padded, steps, *refs),
        out_shape=jax.ShapeDtypeStruct((groups, rows_padded, LANES), jnp.float32),
        grid=(groups,),
        in_specs=[
            pl.BlockSpec((1, total_rows, LANES), lambda g: (g, 0, 0)),
            pl.BlockSpec((1, steps, LANES, LANES), lambda g: (g, 0, 0, 0)),
        ],
        out_specs=pl.BlockSpec((1, rows_padded, LANES), lambda g: (g, 0, 0)),
        compiler_params=pltpu.CompilerParams(vmem_limit_bytes=40 * 1024 * 1024),
    )(spread, matrix)
    biases = jnp.tile(position_bias.reshape(groups, 1, width), (1, 1, PHASES))
    position = jax.nn.gelu(response[:, :rows, :inner] + biases, approximate=False)
    position = position.astype(jnp.bfloat16).reshape(groups, rows * PHASES, width)
    return position[:, :frames].transpose(1, 0, 2).reshape(frames, channels)


PER_STEP = 2


def attention_kernel(listed, scale, ids_ref, mask_ref, q_ref, k_ref, v_ref, o_ref):
    for place in range(PER_STEP):
        row = pl.program_id(0) * PER_STEP + place
        queries = q_ref[place * BLOCK : (place + 1) * BLOCK, :]
        scores, values = [], []
        for at in range(listed):
            begin = pl.multiple_of(ids_ref[row, at] * BLOCK, BLOCK)
            score = lax.dot_general(
                queries,
                k_ref[pl.ds(begin, BLOCK), :],
                (((1,), (1,)), ((), ())),
                preferred_element_type=jnp.float32,
            )
            scores.append(jnp.where(mask_ref[row, at] > 0, score * scale, -jnp.inf))
            values.append(v_ref[pl.ds(begin, BLOCK), :])
        peak = scores[0]
        for score in scores[1:]:
            peak = jnp.maximum(peak, score)
        peak = jnp.max(peak, axis=1, keepdims=True)
        weights = [jnp.exp(score - peak) for score in scores]
        total = weights[0]
        for weight in weights[1:]:
            total = total + weight
        total = jnp.sum(total, axis=1, keepdims=True)
        probability = jnp.concatenate(
            [weight.astype(jnp.bfloat16) for weight in weights], axis=1
        )
        context = jnp.dot(
            probability, jnp.concatenate(values, axis=0), preferred_element_type=jnp.float32
        )
        o_ref[place * BLOCK : (place + 1) * BLOCK, :] = (context / total).astype(jnp.bfloat16)


def attend_head(queries, keys, values, block_ids, allowed):
    frames, width = queries.shape
    blocks, listed = block_ids.shape
    whole = pl.BlockSpec((frames, width), lambda b, *_: (0, 0))
    tile = pl.BlockSpec((PER_STEP * BLOCK, width), lambda b, *_: (b, 0))
    return pl.pallas_call(
        lambda *refs: attention_kernel(listed, 1.0 / math.sqrt(HEAD), *refs),
        out_shape=jax.ShapeDtypeStruct((frames, width), jnp.bfloat16),
        grid_spec=pltpu.PrefetchScalarGridSpec(
            num_scalar_prefetch=2,
            grid=(blocks // PER_STEP,),
            in_specs=[tile, whole, whole],
            out_specs=tile,
        ),
    )(block_ids, allowed, queries, keys, values)


def by_heads(
    signal,
    position_kernel,
    position_bias,
    layer_gain,
    layer_shift,
    query_weight,
    query_bias,
    key_weight,
    value_weight,
    value_bias,
    output_weight,
    output_bias,
    key_blocks,
    global_blocks,
):
    records = lax.axis_size("rec")
    record = lax.axis_index("rec")
    part = query_weight.shape[0] // records
    inner = HEADS * HEAD
    rows = [
        lax.dynamic_slice_in_dim(weight, record * part, part, axis=0)
        for weight in (query_weight, key_weight, value_weight)
    ]
    rows = jnp.stack(rows, axis=1).reshape(part, 3, HEADS, HEAD).transpose(0, 2, 1, 3)
    output_rows = lax.dynamic_slice_in_dim(output_weight, record * part, part, axis=1).T
    incoming = lax.all_to_all(signal, "tm", split_axis=1, concat_axis=0, tiled=True)
    weights = lax.all_gather(rows.reshape(part, 3 * inner), ("tm", "rec"), axis=0, tiled=True)
    output_rows, incoming = lax.optimization_barrier((output_rows, incoming))
    output_weights = lax.all_gather(output_rows, ("tm", "rec"), axis=0, tiled=True)
    listed = lax.all_gather(key_blocks, "tm", axis=0, tiled=True)
    position = position_term(incoming, position_kernel, position_bias)
    returned = lax.all_to_all(position, "tm", split_axis=0, concat_axis=1, tiled=True)
    hidden = signal.astype(jnp.float32) + returned.astype(jnp.float32)
    average = jnp.mean(hidden, axis=-1, keepdims=True)
    centered = hidden - average
    variance = jnp.mean(centered * centered, axis=-1, keepdims=True)
    normed = (centered * lax.rsqrt(variance + EPSILON) * layer_gain + layer_shift).astype(
        jnp.bfloat16
    )
    biases = jnp.stack((query_bias, jnp.zeros_like(query_bias), value_bias))
    biases = biases.reshape(3, HEADS, HEAD).transpose(1, 0, 2).reshape(-1)
    projected = jnp.dot(normed, weights, preferred_element_type=jnp.float32)
    projected = (projected + biases).astype(jnp.bfloat16)
    headed = lax.all_to_all(projected, "tm", split_axis=1, concat_axis=0, tiled=True)
    blocks = listed.shape[0]
    repeated = jnp.any(global_blocks[None, :, None] == listed[:, None, :], axis=-1)
    block_ids = jnp.concatenate(
        [jnp.maximum(listed, 0), jnp.broadcast_to(global_blocks[None, :], (blocks, GLOBALS))],
        axis=1,
    )
    allowed = jnp.concatenate([listed >= 0, jnp.logical_not(repeated)], axis=1)
    context = attend_head(
        headed[:, :HEAD],
        headed[:, HEAD : 2 * HEAD],
        headed[:, 2 * HEAD :],
        block_ids,
        allowed.astype(jnp.int32),
    )
    context = lax.all_to_all(context, "tm", split_axis=0, concat_axis=1, tiled=True)
    projected = lax.dot_general(
        context,
        output_weights,
        (((1,), (1,)), ((), ())),
        preferred_element_type=jnp.float32,
    )
    return (hidden + projected + output_bias).astype(jnp.bfloat16)


def body(*operands):
    share, width, _ = operands[1].shape
    fits = lax.axis_size("tm") == HEADS and share % width == 0
    fits = fits and operands[5].shape[0] % lax.axis_size("rec") == 0
    return (by_heads if fits else general)(*operands)


def solution(mesh):
    placed = (
        P(("rec", "tm"), None),
        P("tm", None, None),
        P("tm"),
        P(),
        P(),
        P("tm", None),
        P(),
        P("tm", None),
        P("tm", None),
        P(),
        P(None, "tm"),
        P(),
        P(("rec", "tm"), None),
        P("rec"),
    )
    return jax.shard_map(
        body, mesh=mesh, in_specs=placed, out_specs=P(("rec", "tm"), None), check_vma=False
    )
```

```python
import math

import jax
import jax.numpy as jnp
import numpy as np
from jax import lax
from jax.experimental import pallas as pl
from jax.experimental.pallas import tpu as pltpu
from jax.sharding import PartitionSpec as P

HEAD = 80
HEADS = 8
BLOCK = 128
GLOBALS = 4


EPSILON = 1e-05


def attend(queries, key_rows, value_rows, allowed):
    block_count, row_count, heads_width = queries.shape
    query_heads = queries.reshape(block_count, row_count, HEADS, HEAD)
    key_heads = key_rows.reshape(block_count, key_rows.shape[1], HEADS, HEAD)
    value_heads = value_rows.reshape(block_count, value_rows.shape[1], HEADS, HEAD)
    scores = jnp.einsum(
        "bqhe,bkhe->bhqk", query_heads, key_heads, preferred_element_type=jnp.float32
    ) * (1.0 / math.sqrt(HEAD))
    scores = jnp.where(allowed[:, None, None, :], scores, -jnp.inf)
    row_max = jnp.max(scores, axis=-1, keepdims=True)
    weights = jnp.exp(scores - row_max)
    row_total = jnp.sum(weights, axis=-1)
    probability = weights.astype(jnp.bfloat16)
    context_sum = jnp.einsum(
        "bhqk,bkhe->bqhe", probability, value_heads, preferred_element_type=jnp.float32
    )
    context = context_sum / jnp.transpose(row_total, (0, 2, 1))[..., None]
    return context.reshape(block_count, row_count, heads_width).astype(jnp.bfloat16)


def general(
    signal,
    position_kernel,
    position_bias,
    layer_gain,
    layer_shift,
    query_weight,
    query_bias,
    key_weight,
    value_weight,
    value_bias,
    output_weight,
    output_bias,
    key_blocks,
    global_blocks,
):
    devices = lax.axis_size("tm")
    frame_count, model_width = signal.shape
    channel_share, group_width, kernel_taps = position_kernel.shape
    inner_width = max(channel_share, group_width)
    folded = signal.T
    if channel_share >= group_width:
        outgoing = folded.reshape(devices, channel_share, frame_count)
    else:
        start_groups = np.arange(devices) * channel_share // group_width
        outgoing = jnp.take(
            folded.reshape(model_width // group_width, group_width, frame_count),
            start_groups,
            axis=0,
        )
    incoming = lax.all_to_all(outgoing, "tm", split_axis=0, concat_axis=2, tiled=True)
    response = lax.conv_general_dilated(
        incoming,
        position_kernel,
        (1,),
        [(kernel_taps // 2, kernel_taps // 2 - 1)],
        dimension_numbers=("NCH", "OIH", "NCH"),
        feature_group_count=inner_width // group_width,
        preferred_element_type=jnp.float32,
    )[0]
    position = jax.nn.gelu(response + position_bias[:, None], approximate=False).astype(
        jnp.bfloat16
    )
    returned = lax.all_to_all(position, "tm", split_axis=1, concat_axis=0, tiled=True)
    hidden = signal.astype(jnp.float32) + returned.T.astype(jnp.float32)
    average = jnp.mean(hidden, axis=-1, keepdims=True)
    centered = hidden - average
    variance = jnp.mean(centered * centered, axis=-1, keepdims=True)
    normed = (centered * lax.rsqrt(variance + EPSILON) * layer_gain + layer_shift).astype(
        jnp.bfloat16
    )
    heads_width = query_weight.shape[1]
    zero_sums = jnp.zeros((frame_count, heads_width), jnp.float32)
    totals = (zero_sums, zero_sums, zero_sums)
    pieces = (
        lax.all_gather(query_weight, "tm", axis=0, tiled=True),
        lax.all_gather(key_weight, "tm", axis=0, tiled=True),
        lax.all_gather(value_weight, "tm", axis=0, tiled=True),
    )
    columns = lax.slice_in_dim(normed, 0, pieces[0].shape[0], axis=1)
    query_sum, key_sum, value_sum = tuple(
        (
            running + jnp.dot(columns, weight_rows, preferred_element_type=jnp.float32)
            for running, weight_rows in zip(totals, pieces)
        )
    )
    queries = (query_sum + query_bias).astype(jnp.bfloat16)
    key_part = key_sum.astype(jnp.bfloat16)
    value_part = (value_sum + value_bias).astype(jnp.bfloat16)
    key_value = jnp.stack((key_part, value_part), axis=1)
    per_device = frame_count // BLOCK
    repeated = jnp.any(global_blocks[None, :, None] == key_blocks[:, None, :], axis=-1)
    whole = lax.all_gather(key_value, "tm", axis=0, tiled=True)
    block_ids = jnp.concatenate(
        [key_blocks, jnp.broadcast_to(global_blocks[None, :], (per_device, GLOBALS))], axis=1
    )
    allowed = jnp.concatenate([key_blocks >= 0, jnp.logical_not(repeated)], axis=1)
    candidates = whole.reshape(-1, BLOCK, 2, heads_width)[jnp.maximum(block_ids, 0)]
    key_rows = candidates[:, :, :, 0].reshape(per_device, -1, heads_width)
    value_rows = candidates[:, :, :, 1].reshape(per_device, -1, heads_width)
    allowed_rows = jnp.repeat(allowed, BLOCK, axis=1)
    context = attend(
        queries.reshape(per_device, BLOCK, heads_width), key_rows, value_rows, allowed_rows
    ).reshape(frame_count, heads_width)
    projected = jnp.dot(
        context,
        lax.all_gather(output_weight, "tm", axis=1, tiled=True),
        preferred_element_type=jnp.float32,
    )
    return (hidden + projected + output_bias).astype(jnp.bfloat16)


PHASES = 3
LANES = 256
STEP = 4


def expand_kernel(taps, width, shift, steps, k_ref, o_ref):
    inner = PHASES * width
    for step in range(steps):
        columns = []
        for phase in range(PHASES):
            begin = step * PHASES - phase - shift
            low = min(max(begin, 0), taps)
            high = min(max(begin + PHASES, 0), taps)
            pieces = []
            if low > begin and high > low:
                pieces.append(jnp.zeros(((low - begin) * width, width), jnp.bfloat16))
            if high > low:
                pieces.append(k_ref[0, low * width : high * width, :])
            missing = inner - sum(piece.shape[0] for piece in pieces)
            if missing:
                pieces.append(jnp.zeros((missing, width), jnp.bfloat16))
            columns.append(pieces[0] if len(pieces) == 1 else jnp.concatenate(pieces, axis=0))
        columns.append(jnp.zeros((inner, LANES - inner), jnp.bfloat16))
        o_ref[0, step, :inner, :] = jnp.concatenate(columns, axis=1)
        o_ref[0, step, inner:, :] = jnp.zeros((LANES - inner, LANES), jnp.bfloat16)


def conv_kernel(rows, steps, x_ref, w_ref, b_ref, o_ref, total_ref):
    total_ref[...] = jnp.zeros_like(total_ref)

    for step in range(0, steps, STEP):
        window = jnp.concatenate(
            [
                x_ref[0, step + at : step + at + rows, :].astype(jnp.bfloat16)
                for at in range(STEP)
            ],
            axis=1,
        )
        taps = w_ref[0, step : step + STEP].reshape(STEP * LANES, LANES)
        total_ref[...] += jnp.dot(window, taps, preferred_element_type=jnp.float32)
    value = total_ref[...] + b_ref[0]
    gelu = value * (1.0 + lax.erf(value * (0.5**0.5))) * 0.5
    o_ref[0] = gelu.astype(jnp.bfloat16)


def position_term(incoming, position_kernel, position_bias):
    frames, channels = incoming.shape
    _, width, taps = position_kernel.shape
    groups = channels // width
    reach = taps // 2
    lead = -(-reach // PHASES)
    shift = lead * PHASES - reach
    steps = -(-(taps + shift + PHASES - 1) // (PHASES * STEP)) * STEP
    rows = -(-frames // PHASES)
    rows_padded = -(-rows // 16) * 16
    total_rows = -(-(rows_padded + steps) // 8) * 8
    front = lead * PHASES
    inner = PHASES * width
    spread = jnp.pad(incoming, ((front, total_rows * PHASES - front - frames), (0, 0)))
    spread = spread.reshape(total_rows, PHASES, groups, width)
    spread = spread.transpose(2, 0, 1, 3).reshape(groups, total_rows, inner)
    spread = jnp.pad(spread, ((0, 0), (0, 0), (0, LANES - inner))).astype(jnp.float32)
    kernels = position_kernel.reshape(groups, width, width, taps).transpose(0, 3, 2, 1)
    kernels = kernels.reshape(groups, taps * width, width)
    matrix = pl.pallas_call(
        lambda *refs: expand_kernel(taps, width, shift, steps, *refs),
        out_shape=jax.ShapeDtypeStruct((groups, steps, LANES, LANES), jnp.bfloat16),
        grid=(groups,),
        in_specs=[pl.BlockSpec((1, taps * width, width), lambda g: (g, 0, 0))],
        out_specs=pl.BlockSpec((1, steps, LANES, LANES), lambda g: (g, 0, 0, 0)),
        compiler_params=pltpu.CompilerParams(vmem_limit_bytes=56 * 1024 * 1024),
    )(kernels)
    biases = jnp.tile(position_bias.reshape(groups, 1, width), (1, 1, PHASES))
    biases = jnp.pad(biases, ((0, 0), (0, 0), (0, LANES - inner)))
    position = pl.pallas_call(
        lambda *refs: conv_kernel(rows_padded, steps, *refs),
        out_shape=jax.ShapeDtypeStruct((groups, rows_padded, LANES), jnp.bfloat16),
        grid=(groups,),
        in_specs=[
            pl.BlockSpec((1, total_rows, LANES), lambda g: (g, 0, 0)),
            pl.BlockSpec((1, steps, LANES, LANES), lambda g: (g, 0, 0, 0)),
            pl.BlockSpec((1, 1, LANES), lambda g: (g, 0, 0)),
        ],
        out_specs=pl.BlockSpec((1, rows_padded, LANES), lambda g: (g, 0, 0)),
        scratch_shapes=[pltpu.VMEM((rows_padded, LANES), jnp.float32)],
        compiler_params=pltpu.CompilerParams(vmem_limit_bytes=56 * 1024 * 1024),
    )(spread, matrix, biases)
    position = position[:, :rows, :inner].reshape(groups, rows * PHASES, width)
    return position[:, :frames].transpose(1, 0, 2).reshape(frames, channels)


PER_STEP = 4


def attention_kernel(listed, scale, ids_ref, mask_ref, q_ref, k_ref, v_ref, o_ref):
    for place in range(PER_STEP):
        row = pl.program_id(0) * PER_STEP + place
        queries = q_ref[place * BLOCK : (place + 1) * BLOCK, :]
        scores, values = [], []
        for at in range(listed):
            begin = pl.multiple_of(ids_ref[row, at] * BLOCK, BLOCK)
            score = lax.dot_general(
                queries,
                k_ref[pl.ds(begin, BLOCK), :],
                (((1,), (1,)), ((), ())),
                preferred_element_type=jnp.float32,
            )
            scores.append(jnp.where(mask_ref[row, at] > 0, score * scale, -jnp.inf))
            values.append(v_ref[pl.ds(begin, BLOCK), :])
        peak = scores[0]
        for score in scores[1:]:
            peak = jnp.maximum(peak, score)
        peak = jnp.max(peak, axis=1, keepdims=True)
        weights = [jnp.exp(score - peak) for score in scores]
        total = weights[0]
        for weight in weights[1:]:
            total = total + weight
        total = jnp.sum(total, axis=1, keepdims=True)
        probability = jnp.concatenate(
            [weight.astype(jnp.bfloat16) for weight in weights], axis=1
        )
        context = jnp.dot(
            probability, jnp.concatenate(values, axis=0), preferred_element_type=jnp.float32
        )
        o_ref[place * BLOCK : (place + 1) * BLOCK, :] = (context / total).astype(jnp.bfloat16)


def attend_head(queries, keys, values, block_ids, allowed):
    frames, width = queries.shape
    blocks, listed = block_ids.shape
    whole = pl.BlockSpec((frames, width), lambda b, *_: (0, 0))
    tile = pl.BlockSpec((PER_STEP * BLOCK, width), lambda b, *_: (b, 0))
    return pl.pallas_call(
        lambda *refs: attention_kernel(listed, 1.0 / math.sqrt(HEAD), *refs),
        out_shape=jax.ShapeDtypeStruct((frames, width), jnp.bfloat16),
        grid_spec=pltpu.PrefetchScalarGridSpec(
            num_scalar_prefetch=2,
            grid=(blocks // PER_STEP,),
            in_specs=[tile, whole, whole],
            out_specs=tile,
        ),
    )(block_ids, allowed, queries, keys, values)


def by_heads(
    signal,
    position_kernel,
    position_bias,
    layer_gain,
    layer_shift,
    query_weight,
    query_bias,
    key_weight,
    value_weight,
    value_bias,
    output_weight,
    output_bias,
    key_blocks,
    global_blocks,
):
    records = lax.axis_size("rec")
    record = lax.axis_index("rec")
    part = query_weight.shape[0] // records
    inner = HEADS * HEAD
    rows = [
        lax.dynamic_slice_in_dim(weight, record * part, part, axis=0)
        for weight in (query_weight, key_weight, value_weight)
    ]
    rows = jnp.stack(rows, axis=1).reshape(part, 3, HEADS, HEAD).transpose(0, 2, 1, 3)
    output_rows = lax.dynamic_slice_in_dim(output_weight, record * part, part, axis=1).T
    incoming = lax.all_to_all(signal, "tm", split_axis=1, concat_axis=0, tiled=True)
    weights = lax.all_gather(rows.reshape(part, 3 * inner), ("tm", "rec"), axis=0, tiled=True)
    output_rows, incoming = lax.optimization_barrier((output_rows, incoming))
    output_weights = lax.all_gather(output_rows, ("tm", "rec"), axis=0, tiled=True)
    position = position_term(incoming, position_kernel, position_bias)
    own_list, position = lax.optimization_barrier((key_blocks, position))
    listed = lax.all_gather(own_list, "tm", axis=0, tiled=True)
    returned = lax.all_to_all(position, "tm", split_axis=0, concat_axis=1, tiled=True)
    returned, listed = lax.optimization_barrier((returned, listed))
    hidden = signal.astype(jnp.float32) + returned.astype(jnp.float32)
    average = jnp.mean(hidden, axis=-1, keepdims=True)
    centered = hidden - average
    variance = jnp.mean(centered * centered, axis=-1, keepdims=True)
    normed = (centered * lax.rsqrt(variance + EPSILON) * layer_gain + layer_shift).astype(
        jnp.bfloat16
    )
    biases = jnp.stack((query_bias, jnp.zeros_like(query_bias), value_bias))
    biases = biases.reshape(3, HEADS, HEAD).transpose(1, 0, 2).reshape(-1)
    projected = jnp.dot(normed, weights, preferred_element_type=jnp.float32)
    projected = (projected + biases).astype(jnp.bfloat16)
    headed = lax.all_to_all(projected, "tm", split_axis=1, concat_axis=0, tiled=True)
    blocks = listed.shape[0]
    repeated = jnp.any(global_blocks[None, :, None] == listed[:, None, :], axis=-1)
    block_ids = jnp.concatenate(
        [jnp.maximum(listed, 0), jnp.broadcast_to(global_blocks[None, :], (blocks, GLOBALS))],
        axis=1,
    )
    allowed = jnp.concatenate([listed >= 0, jnp.logical_not(repeated)], axis=1)
    context = attend_head(
        headed[:, :HEAD],
        headed[:, HEAD : 2 * HEAD],
        headed[:, 2 * HEAD :],
        block_ids,
        allowed.astype(jnp.int32),
    )
    context = lax.all_to_all(context, "tm", split_axis=0, concat_axis=1, tiled=True)
    projected = lax.dot_general(
        context,
        output_weights,
        (((1,), (1,)), ((), ())),
        preferred_element_type=jnp.float32,
    )
    return (hidden + projected + output_bias).astype(jnp.bfloat16)


def body(*operands):
    share, width, _ = operands[1].shape
    fits = lax.axis_size("tm") == HEADS and share % width == 0
    fits = fits and operands[5].shape[0] % lax.axis_size("rec") == 0
    return (by_heads if fits else general)(*operands)


def solution(mesh):
    placed = (
        P(("rec", "tm"), None),
        P("tm", None, None),
        P("tm"),
        P(),
        P(),
        P("tm", None),
        P(),
        P("tm", None),
        P("tm", None),
        P(),
        P(None, "tm"),
        P(),
        P(("rec", "tm"), None),
        P("rec"),
    )
    return jax.shard_map(
        body, mesh=mesh, in_specs=placed, out_specs=P(("rec", "tm"), None), check_vma=False
    )
```
